512 devices in a mesh: tile: 16 (over z, core), depth: 32 (over y, x).
Axes of the slice: x: 4, y: 8, z: 8, core: 2. Of those that a mesh axis runs over, the one named last changes fastest.
Arguments:
- velocity: float32 [3, 512, 96, 2048], P(None, 'depth', None, 'tile'), may hold values from -6 to 6
- metric: float32 [96], replicated, may hold values from 0.5 to 2
- colour_map: bfloat16 [4, 128], replicated, may hold values from 0.049804688 to 1
- counts: int32 [96, 2048], P(None, 'tile'), may hold values from 1 to 512
Outputs:
- rendered: float32 [4, 96, 2048], P(None, 'depth', 'tile')
The draws below stay inside these ranges and needn't reach their ends.
Inputs may be any that keep to these rules, and one draw needn't show every extreme that they name: `counts`: each pixel's ray passes the cells with z below its count.
All inputs are finite; a program needn't handle non-finite values.
Results may differ from the reference program's by a relative error of at most 0.0003.
Values sent between devices are 32-bit elements; how exact they have to be, the bound alone decides.
A program may use at most 64 MiB of HBM per device.

```python
import math
import jax
import jax.numpy as jnp
from jax import lax

CX = 128
NY = 96
NBINS = 128
NX = 2048
NZ = 512
N_TILE = 16


def with_ends(drawn, key, low, top_value):
    longest = drawn.shape.index(max(drawn.shape))
    spots = []
    for shift in (0, 1):
        where = [jax.random.randint(jax.random.fold_in(key, axis), (), 0, length) for axis, length in enumerate(drawn.shape)]
        where[longest] = (where[longest] + shift) % drawn.shape[longest]
        spots.append(tuple(where))
    return drawn.at[spots[0]].set(low).at[spots[1]].set(top_value)


def level_of(rng, dims, pieces, smallest, largest):
    loudness, own = 1.0, jax.random.fold_in(rng, 6)
    for position, parts in pieces:
        steps = jnp.exp(jax.random.uniform(jax.random.fold_in(own, position), (parts,), jnp.float32, smallest / len(pieces), largest / len(pieces)))
        loudness = loudness * jnp.repeat(steps, dims[position] // parts).reshape([-1 if axis == position else 1 for axis in range(len(dims))])
    return loudness


def bell_draw(key, shape, deviation, bound, cuts=(), kind=jnp.bfloat16):
    gain = level_of(key, shape, cuts, -0.22, 0.18) if cuts else 1.0
    drawn = jax.random.normal(key, shape, jnp.float32) * deviation * gain
    return jnp.minimum(jnp.maximum(drawn, -bound), bound).astype(kind)


def setup_inputs(seed: int = 0) -> dict:
    streams_of = jax.random.split(jax.random.key(seed), 5)
    velocity = bell_draw(streams_of[0], (3, NZ, NY, NX), 1.0, 6.0, ((1, 32), (3, 16)), jnp.float32)
    metric = jnp.clip(jnp.exp(jax.random.uniform(streams_of[1], (NY,), jnp.float32, math.log(0.5), math.log(2.0))), 0.5, 2.0)
    colour_map = jnp.clip(jax.random.uniform(streams_of[2], (4, NBINS), jnp.float32, 0.049804688, 1.0), 0.049804688, 1.0).astype(jnp.bfloat16)
    counts = with_ends(jax.random.randint(streams_of[3], (NY, NX), 1, NZ + 1), jax.random.fold_in(streams_of[3], 1), 1, NZ).astype(jnp.int32)
    return {"velocity": velocity, "metric": metric, "colour_map": colour_map, "counts": counts}


STENCIL_WEIGHTS = (45.0 / 60.0, -9.0 / 60.0, 1.0 / 60.0)
CRITERION_SCALE = 2.0
VORTEX_SCALE = 4.0
OPTICAL_DEPTH = 4.0

def interior(padded, keep_dim):
    for dimension in range(3):
        if dimension != keep_dim:
            padded = lax.slice_in_dim(padded, 3, padded.shape[dimension] - 3, axis=dimension)
    return padded

def central(padded, dimension):
    extent = padded.shape[dimension] - 6
    result = None
    for offset, weight in zip((1, 2, 3), STENCIL_WEIGHTS):
        forward = lax.slice_in_dim(padded, 3 + offset, 3 + offset + extent, axis=dimension)
        backward = lax.slice_in_dim(padded, 3 - offset, 3 - offset + extent, axis=dimension)
        result = weight * (forward - backward) if result is None else result + weight * (forward - backward)
    return result

def gradients(padded, metric_rows):
    tensor = []
    for component in range(3):
        component_field = padded[component]
        stream_slope = central(interior(component_field, 2), 2)
        normal_slope = central(interior(component_field, 1), 1) * metric_rows[None, :, None]
        span_slope = central(interior(component_field, 0), 0)
        tensor.append((stream_slope, normal_slope, span_slope))
    return tensor

def invariants(tensor):
    contraction = jnp.zeros_like(tensor[0][0])
    for source in range(3):
        for target in range(3):
            contraction = contraction + tensor[source][target] * tensor[target][source]
    curl_first = tensor[2][1] - tensor[1][2]
    curl_second = tensor[0][2] - tensor[2][0]
    curl_third = tensor[1][0] - tensor[0][1]
    vortex = jnp.sqrt(curl_first * curl_first + curl_second * curl_second + curl_third * curl_third)
    return (-0.5 * contraction, vortex)

def reference(velocity, metric, colour_map, counts):
    map_float = colour_map.astype(jnp.float32)

    def render_block(block_start):
        columns = (block_start - 3 + jnp.arange(CX + 6, dtype=jnp.int32)) % NX
        section = jnp.take(velocity, columns, axis=3)
        section = jnp.pad(section, ((0, 0), (3, 3), (0, 0), (0, 0)), mode='wrap')
        section = jnp.pad(section, ((0, 0), (0, 0), (3, 3), (0, 0)))
        criterion, vortex = invariants(gradients(section, metric))
        bin_level = (NBINS - 1) * 0.5 * (1.0 + jnp.tanh(criterion / CRITERION_SCALE))
        lowbin = jnp.minimum(jnp.floor(bin_level), NBINS - 2).astype(jnp.int32)
        fraction = bin_level - lowbin.astype(bin_level.dtype)
        lower_value = jnp.take(map_float, lowbin, axis=1)
        upper_value = jnp.take(map_float, lowbin + 1, axis=1)
        values = (1.0 - fraction) * lower_value + fraction * upper_value
        count_block = lax.dynamic_slice_in_dim(counts, block_start, CX, 1)
        depth_index = jnp.arange(NZ, dtype=jnp.int32)[:, None, None]
        inside = depth_index < count_block[None]
        extinct = jnp.where(inside, values[0] * (OPTICAL_DEPTH / NZ), jnp.zeros_like(values[0]))
        opacity = -jnp.expm1(-extinct)
        emission = values[1:] * jnp.tanh(vortex / VORTEX_SCALE)[None]
        before = jnp.cumsum(extinct, axis=0) - extinct
        colour = lax.optimization_barrier(jnp.sum((jnp.exp(-before) * opacity)[None] * emission, axis=1))
        total = lax.optimization_barrier(jnp.sum(extinct, axis=0))
        return jnp.concatenate([colour, -jnp.expm1(-total)[None]], axis=0)
    block_starts = jnp.arange(N_TILE, dtype=jnp.int32) * CX
    stacked = lax.map(render_block, block_starts)
    return jnp.transpose(stacked, (1, 2, 0, 3)).reshape(4, NY, NX)
```

```python
import functools

import jax
import jax.numpy as jnp
import numpy as np
from jax import lax
from jax.experimental import pallas as pl
from jax.experimental.pallas import tpu as pltpu
from jax.sharding import PartitionSpec as P

COEF = {1: 45.0, -1: -45.0, 2: -9.0, -2: 9.0, 3: 1.0, -3: -1.0}
VORTEX_SCALE = 4.0
OPTICAL_DEPTH = 4.0
CHUNKS = 4
MESH = pl.DeviceIdType.MESH


def stencil_tables(planes, rows, lanes):
    along_rows = np.zeros((rows, rows), np.float32)
    for row in range(rows):
        for offset, weight in COEF.items():
            if 0 <= row + offset < rows:
                along_rows[row, row + offset] = weight
    along_rows = np.concatenate([along_rows, along_rows], axis=1)
    along_lanes = np.zeros((planes, 2 * lanes, lanes), np.float32)
    for plane in range(planes):
        for lane in range(lanes):
            for offset, weight in COEF.items():
                source = lane + offset
                if source < 0:
                    place = lanes + 8 * plane + source + 3
                elif source >= lanes:
                    place = lanes + 8 * plane + source - lanes + 3
                else:
                    place = source
                along_lanes[plane, place, lane] = weight
    return along_rows.astype(jnp.bfloat16), along_lanes.astype(jnp.bfloat16)


def kernel(
    depth_count,
    tile_count,
    vel_hbm,
    metric_hbm,
    map_hbm,
    counts_hbm,
    rowtab_hbm,
    lanetab_hbm,
    out_ref,
    vel,
    high,
    low,
    dx,
    dy,
    metric_in,
    metric,
    map_in,
    table,
    counts,
    rowtab,
    lanetab,
    edge,
    from_left,
    from_right,
    stage,
    pieces,
    landed,
    load_sem,
    edge_send,
    edge_recv,
    halo_send,
    halo_recv,
    piece_send,
    piece_recv,
    ready_sem,
):
    slab = vel_hbm.shape[1]
    rows, lanes = vel_hbm.shape[2:]
    chunk_rows = rows // CHUNKS
    owners = depth_count // CHUNKS
    me = lax.axis_index("depth")
    tile = lax.axis_index("tile")
    up, down = lax.rem(me + 1, depth_count), lax.rem(me + depth_count - 1, depth_count)
    right, left = lax.rem(tile + 1, tile_count), lax.rem(tile + tile_count - 1, tile_count)

    barrier = pltpu.get_barrier_semaphore()
    for peer in ({"depth": up}, {"depth": down}, {"tile": right}, {"tile": left}):
        pl.semaphore_signal(barrier, inc=1, device_id=peer, device_id_type=MESH)

    loads = [
        pltpu.make_async_copy(vel_hbm.at[c], vel.at[c, pl.ds(3, slab)], load_sem.at[c])
        for c in range(3)
    ]
    for place, (source, target) in enumerate(
        (
            (rowtab_hbm, rowtab),
            (metric_hbm, metric_in),
            (lanetab_hbm, lanetab),
            (map_hbm, map_in),
            (counts_hbm, counts),
        )
    ):
        loads.append(pltpu.make_async_copy(source, target, load_sem.at[3 + place]))
    for load in loads:
        load.start()

    def chunk_of(device, step):
        own = device // owners
        return lax.rem(own + jnp.where(step == 0, 2, jnp.where(step == 1, 1, jnp.where(step == 2, 3, 0))), CHUNKS)

    def chunk_at(device, step):
        return pl.ds(pl.multiple_of(chunk_of(device, step) * chunk_rows, 8), chunk_rows)

    def halo_copy(step, upward):
        target = up if upward else down
        window = chunk_at(target, step)
        first, place = (slab - 3, 0) if upward else (0, slab + 3)
        return pltpu.make_async_remote_copy(
            src_ref=vel_hbm.at[:, pl.ds(first, 3), window, :],
            dst_ref=vel.at[:, pl.ds(place, 3), window, :],
            send_sem=halo_send.at[int(upward), step],
            recv_sem=halo_recv.at[int(upward), step],
            device_id={"depth": target},
            device_id_type=MESH,
        )

    def halo_arrival(step, upward):
        window = chunk_at(me, step)
        place = 0 if upward else slab + 3
        part = vel.at[:, pl.ds(place, 3), window, :]
        return pltpu.make_async_copy(part, part, halo_recv.at[int(upward), step])

    def greet(level):
        for peer in (
            lax.rem(me + 2**level, depth_count),
            lax.rem(me + depth_count - 2**level, depth_count),
        ):
            pl.semaphore_signal(
                ready_sem.at[level], inc=1, device_id={"depth": peer}, device_id_type=MESH
            )

    pl.semaphore_wait(barrier, 4)
    for step in range(CHUNKS):
        for upward in (True, False):
            halo_copy(step, upward).start()
    greet(0)

    for load in loads[:3]:
        load.wait()

    lane = lax.broadcasted_iota(jnp.int32, (8, lanes), 1)

    def pack(place, carry):
        component = place // (rows // 8)
        window = pl.ds(pl.multiple_of(lax.rem(place, rows // 8) * 8, 8), 8)
        packed = jnp.zeros((8, lanes), jnp.float32)
        for plane in range(slab):
            turned = pltpu.roll(vel[component, 3 + plane, window, :], (8 * plane + 3) % lanes, 1)
            packed = jnp.where(lane // 8 == plane, turned, packed)
        edge[component, window, :] = packed
        return carry

    lax.fori_loop(0, 3 * rows // 8, pack, 0)

    edge_copies = [
        pltpu.make_async_remote_copy(
            src_ref=edge,
            dst_ref=target,
            send_sem=edge_send.at[place],
            recv_sem=edge_recv.at[place],
            device_id={"tile": peer},
            device_id_type=MESH,
        )
        for place, (target, peer) in enumerate(((from_left, right), (from_right, left)))
    ]
    for copy in edge_copies:
        copy.start()

    pl.semaphore_wait(ready_sem.at[0], 2)
    greet(1)

    for load in loads[3:]:
        load.wait()
    diagonal = lax.broadcasted_iota(jnp.int32, (rows, rows), 0) == lax.broadcasted_iota(
        jnp.int32, (rows, rows), 1
    )
    column = jnp.sum(
        jnp.where(diagonal, jnp.broadcast_to(metric_in[...], (rows, rows)), 0.0),
        axis=1,
        keepdims=True,
    )
    metric[...] = jnp.broadcast_to(column, (rows, lanes))
    entries = map_in[...].astype(jnp.float32)
    steps = pltpu.roll(entries, lanes - 1, 1) - entries
    for channel in range(4):
        table[channel] = jnp.broadcast_to(entries[channel : channel + 1], (8, lanes))
        table[4 + channel] = jnp.broadcast_to(steps[channel : channel + 1], (8, lanes))

    def row_slopes(place, carry):
        component, pair = place // (slab // 2), lax.rem(place, slab // 2)
        first = 2 * pair
        both = jnp.concatenate([vel[component, 3 + first], vel[component, 4 + first]], axis=1)
        upper = both.astype(jnp.bfloat16)
        lower = (both - upper.astype(jnp.float32)).astype(jnp.bfloat16)
        slopes = jnp.dot(
            rowtab[...],
            jnp.concatenate([upper, lower], axis=0),
            preferred_element_type=jnp.float32,
        )
        for half in range(2):
            part = slice(half * lanes, (half + 1) * lanes)
            high[component, first + half] = upper[:, part]
            low[component, first + half] = lower[:, part]
            dy[component, first + half] = slopes[:, part] * metric[...]
        return carry

    lax.fori_loop(0, 3 * slab // 2, row_slopes, 0)

    pl.semaphore_wait(ready_sem.at[1], 2)
    greet(2)
    for copy in edge_copies:
        copy.wait()

    wide_lane = lax.broadcasted_iota(jnp.int32, (3, rows, lanes), 2)
    halo = jnp.where(lax.rem(wide_lane, 8) < 3, from_left[...], from_right[...])
    halo_high = halo.astype(jnp.bfloat16)
    edge_high = halo_high.reshape(3 * rows, lanes)
    edge_low = (halo - halo_high.astype(jnp.float32)).astype(jnp.bfloat16).reshape(3 * rows, lanes)

    def lane_slopes(plane, carry):
        weights = lanetab[plane]
        upper = jnp.concatenate([high[:, plane].reshape(3 * rows, lanes), edge_high], axis=1)
        lower = jnp.concatenate([low[:, plane].reshape(3 * rows, lanes), edge_low], axis=1)
        slopes = jnp.dot(upper, weights, preferred_element_type=jnp.float32) + jnp.dot(
            lower, weights, preferred_element_type=jnp.float32
        )
        dx[:, plane] = slopes.reshape(3, rows, lanes)
        return carry

    lax.fori_loop(0, slab, lane_slopes, 0)

    pl.semaphore_wait(ready_sem.at[2], 2)
    greet(3)

    first_cell = me * slab

    def render(window):
        left_over = counts[window, :] - first_cell
        clear = jnp.ones((8, lanes), jnp.float32)
        total = jnp.zeros((8, lanes), jnp.float32)
        colour = [jnp.zeros((8, lanes), jnp.float32) for _ in range(3)]
        for plane in range(slab):
            slope = []
            for component in range(3):
                field = [vel[component, plane + k, window, :] for k in (0, 1, 2, 4, 5, 6)]
                along = (
                    45.0 * (field[3] - field[2]) - 9.0 * (field[4] - field[1]) + (field[5] - field[0])
                )
                slope.append(
                    (dx[component, plane, window, :], dy[component, plane, window, :], along)
                )
            contraction = (
                slope[0][0] * slope[0][0]
                + slope[1][1] * slope[1][1]
                + slope[2][2] * slope[2][2]
                + 2.0
                * (
                    slope[0][1] * slope[1][0]
                    + slope[0][2] * slope[2][0]
                    + slope[1][2] * slope[2][1]
                )
            )
            curl = (
                slope[2][1] - slope[1][2],
                slope[0][2] - slope[2][0],
                slope[1][0] - slope[0][1],
            )
            square = curl[0] * curl[0] + curl[1] * curl[1] + curl[2] * curl[2]
            swirl = jnp.tanh(
                square * lax.rsqrt(jnp.maximum(square, 1e-30)) * (1.0 / (60.0 * VORTEX_SCALE))
            )
            scale = 0.5 * (lanes - 1)
            level = scale + scale * jnp.tanh(contraction * (-1.0 / (4.0 * 3600.0)))
            bins = jnp.minimum(level.astype(jnp.int32), lanes - 2)
            fraction = level - bins.astype(jnp.float32)
            values = [
                jnp.take_along_axis(table[channel], bins, axis=1, mode="promise_in_bounds")
                + fraction
                * jnp.take_along_axis(table[4 + channel], bins, axis=1, mode="promise_in_bounds")
                for channel in range(4)
            ]
            extinct = jnp.where(
                left_over > plane, values[0] * (OPTICAL_DEPTH / (slab * depth_count)), 0.0
            )
            opacity = extinct * (
                1.0 - extinct * (0.5 - extinct * (1.0 / 6.0 - extinct * (1.0 / 24.0)))
            )
            weight = clear * opacity
            clear = clear - weight
            total = total + extinct
            weight = weight * swirl
            colour = [colour[k] + weight * values[1 + k] for k in range(3)]
        return colour + [total]

    def piece_copy(owner):
        return pltpu.make_async_remote_copy(
            src_ref=pieces.at[owner],
            dst_ref=landed.at[me],
            send_sem=piece_send.at[owner],
            recv_sem=piece_recv.at[me],
            device_id={"depth": owner},
            device_id_type=MESH,
        )

    def render_chunk(step, carry):
        for upward in (True, False):
            halo_arrival(step, upward).wait()
        chunk = chunk_of(me, step)

        def render_rows(part, carry):
            window = pl.ds(pl.multiple_of(chunk * chunk_rows + part * 8, 8), 8)
            for channel, image in enumerate(render(window)):
                stage[channel, pl.ds(pl.multiple_of(part * 8, 8), 8), :] = image
            return carry

        lax.fori_loop(0, chunk_rows // 8, render_rows, 0)
        for row in range(3):
            for channel in range(4):
                spread = stage.at[channel][pl.ds(row, owners, stride=3), :]
                for owner in range(owners):
                    pieces[chunk * owners + owner, pl.ds(4 * row + channel, 1), :] = spread[
                        owner : owner + 1
                    ]

        @pl.when(step == 0)
        def _():
            pl.semaphore_wait(ready_sem.at[3], 2)

        def send(place, carry):
            owner = chunk * owners + place

            @pl.when(owner != me)
            def _():
                piece_copy(owner).start()

            return carry

        lax.fori_loop(0, owners, send, 0)
        return carry

    lax.fori_loop(0, CHUNKS, render_chunk, 0)
    landed[me] = pieces[me]

    def receive(place, carry):
        @pl.when(place != me)
        def _():
            pltpu.make_async_copy(landed.at[place], landed.at[place], piece_recv.at[place]).wait()

        return carry

    lax.fori_loop(0, depth_count, receive, 0)

    before = jnp.zeros((3, lanes), jnp.float32)
    colour = [jnp.zeros((3, lanes), jnp.float32) for _ in range(3)]
    for device in range(depth_count):
        part = [landed.at[device][pl.ds(channel, 3, stride=4), :] for channel in range(4)]
        clear = jnp.exp(-before)
        colour = [colour[k] + clear * part[k] for k in range(3)]
        before = before + part[3]
    for channel, image in enumerate(colour + [before]):
        out_ref[channel] = image

    def sent(place, carry):
        @pl.when(place != me)
        def _():
            piece_copy(place).wait_send()

        return carry

    lax.fori_loop(0, depth_count, sent, 0)
    for step in range(CHUNKS):
        for upward in (True, False):
            halo_copy(step, upward).wait_send()


def per_device(depth_count, tile_count, velocity, metric, colour_map, counts):
    slab, rows, lanes = velocity.shape[1:]
    row_table, lane_table = stencil_tables(slab, rows, lanes)
    f32, bf16 = jnp.float32, jnp.bfloat16
    operands = (
        velocity,
        metric.reshape(1, rows),
        colour_map,
        counts,
        jnp.asarray(row_table),
        jnp.asarray(lane_table),
    )
    result = pl.pallas_call(
        functools.partial(kernel, depth_count, tile_count),
        out_shape=jax.ShapeDtypeStruct((4, rows // depth_count, lanes), f32),
        in_specs=[pl.BlockSpec(memory_space=pl.ANY)] * len(operands),
        out_specs=pl.BlockSpec(memory_space=pltpu.VMEM),
        scratch_shapes=[
            pltpu.VMEM((3, slab + 6, rows, lanes), f32),
            pltpu.VMEM((3, slab, rows, lanes), bf16),
            pltpu.VMEM((3, slab, rows, lanes), bf16),
            pltpu.VMEM((3, slab, rows, lanes), f32),
            pltpu.VMEM((3, slab, rows, lanes), f32),
            pltpu.VMEM((1, rows), f32),
            pltpu.VMEM((rows, lanes), f32),
            pltpu.VMEM(colour_map.shape, bf16),
            pltpu.VMEM((8, 8, lanes), f32),
            pltpu.VMEM((rows, lanes), jnp.int32),
            pltpu.VMEM(row_table.shape, bf16),
            pltpu.VMEM(lane_table.shape, bf16),
            pltpu.VMEM((3, rows, lanes), f32),
            pltpu.VMEM((3, rows, lanes), f32),
            pltpu.VMEM((3, rows, lanes), f32),
            pltpu.VMEM((4, rows // CHUNKS, lanes), f32),
            pltpu.VMEM((depth_count, 16, lanes), f32),
            pltpu.VMEM((depth_count, 16, lanes), f32),
            pltpu.SemaphoreType.DMA((8,)),
            pltpu.SemaphoreType.DMA((2,)),
            pltpu.SemaphoreType.DMA((2,)),
            pltpu.SemaphoreType.DMA((2, CHUNKS)),
            pltpu.SemaphoreType.DMA((2, CHUNKS)),
            pltpu.SemaphoreType.DMA((depth_count,)),
            pltpu.SemaphoreType.DMA((depth_count,)),
            pltpu.SemaphoreType.REGULAR((4,)),
        ],
        compiler_params=pltpu.CompilerParams(
            collective_id=0, has_side_effects=True, vmem_limit_bytes=60 * 1024 * 1024
        ),
    )(*operands)
    channel = lax.broadcasted_iota(jnp.int32, result.shape, 0)
    return jnp.where(channel == 3, -jnp.expm1(-result), result)


def solution(mesh):
    in_specs = (P(None, "depth", None, "tile"), P(), P(), P(None, "tile"))
    out_specs = P(None, "depth", "tile")
    return jax.shard_map(
        functools.partial(per_device, mesh.shape["depth"], mesh.shape["tile"]),
        mesh=mesh,
        in_specs=in_specs,
        out_specs=out_specs,
        check_vma=False,
    )
```

```python
import functools

import jax
import jax.numpy as jnp
import numpy as np
from jax import lax
from jax.experimental import pallas as pl
from jax.experimental.pallas import tpu as pltpu
from jax.sharding import PartitionSpec as P

COEF = {1: 45.0, -1: -45.0, 2: -9.0, -2: 9.0, 3: 1.0, -3: -1.0}
VORTEX_SCALE = 4.0
OPTICAL_DEPTH = 4.0
CHUNKS = 4
MESH = pl.DeviceIdType.MESH
ALONG_LANES = lax.GatherDimensionNumbers(
    offset_dims=(),
    collapsed_slice_dims=(1,),
    start_index_map=(1,),
    operand_batching_dims=(0,),
    start_indices_batching_dims=(0,),
)


def stencil_tables(planes, rows, lanes):
    along_rows = np.zeros((rows, rows), np.float32)
    for row in range(rows):
        for offset, weight in COEF.items():
            if 0 <= row + offset < rows:
                along_rows[row, row + offset] = weight
    along_rows = np.concatenate([along_rows, along_rows], axis=1)
    along_lanes = np.zeros((lanes, lanes), np.float32)
    from_halo = np.zeros((planes // 2, lanes, 2 * lanes), np.float32)
    for lane in range(lanes):
        for offset, weight in COEF.items():
            source = lane + offset
            if 0 <= source < lanes:
                along_lanes[source, lane] = weight
                continue
            slot = source + 3 if source < 0 else source - lanes + 3
            for plane in range(planes):
                from_halo[plane // 2, 8 * plane + slot, plane % 2 * lanes + lane] = weight
    return tuple(table.astype(jnp.bfloat16) for table in (along_rows, along_lanes, from_halo))


def lookup(table, bins):
    return lax.gather(
        table,
        bins[..., None],
        ALONG_LANES,
        slice_sizes=(1, 1),
        mode=lax.GatherScatterMode.PROMISE_IN_BOUNDS,
    )


def kernel(
    depth_count,
    tile_count,
    vel_hbm,
    metric_hbm,
    map_hbm,
    counts_hbm,
    rowtab_hbm,
    lanetab_hbm,
    halotab_hbm,
    out_ref,
    vel,
    high,
    low,
    dx,
    dy,
    rest,
    spin,
    span,
    metric_in,
    metric,
    map_in,
    table,
    counts,
    rowtab,
    lanetab,
    halotab,
    edge,
    from_left,
    from_right,
    edge_parts,
    stage,
    pieces,
    landed,
    load_sem,
    edge_send,
    edge_recv,
    halo_send,
    halo_recv,
    piece_send,
    piece_recv,
    ready_sem,
    tile_sem,
):
    slab = vel_hbm.shape[1]
    rows, lanes = vel_hbm.shape[2:]
    chunk_rows = rows // CHUNKS
    owners = depth_count // CHUNKS
    me = lax.axis_index("depth")
    tile = lax.axis_index("tile")
    odd = lax.rem(tile, 2)
    up, down = lax.rem(me + 1, depth_count), lax.rem(me + depth_count - 1, depth_count)
    right, left = lax.rem(tile + 1, tile_count), lax.rem(tile + tile_count - 1, tile_count)

    barrier = pltpu.get_barrier_semaphore()
    for peer in (up, down):
        pl.semaphore_signal(barrier, inc=1, device_id={"depth": peer}, device_id_type=MESH)

    @pl.when(odd == 0)
    def _():
        for peer in (right, left):
            pl.semaphore_signal(barrier, inc=1, device_id={"tile": peer}, device_id_type=MESH)

    loads = [
        pltpu.make_async_copy(vel_hbm.at[c], vel.at[c, pl.ds(3, slab)], load_sem.at[c])
        for c in range(3)
    ]
    for place, (source, target) in enumerate(
        (
            (rowtab_hbm, rowtab),
            (metric_hbm, metric_in),
            (lanetab_hbm, lanetab),
            (map_hbm, map_in),
            (counts_hbm, counts),
            (halotab_hbm, halotab),
        )
    ):
        loads.append(pltpu.make_async_copy(source, target, load_sem.at[3 + place]))
    for load in loads:
        load.start()

    def chunk_of(device, step):
        own = device // owners
        return lax.rem(
            own + jnp.where(step == 0, 2, jnp.where(step == 1, 1, jnp.where(step == 2, 3, 0))),
            CHUNKS,
        )

    def chunk_at(device, step):
        return pl.ds(pl.multiple_of(chunk_of(device, step) * chunk_rows, 8), chunk_rows)

    def halo_copy(step, upward):
        target = up if upward else down
        window = chunk_at(target, step)
        first, place = (slab - 3, 0) if upward else (0, slab + 3)
        return pltpu.make_async_remote_copy(
            src_ref=vel_hbm.at[:, pl.ds(first, 3), window, :],
            dst_ref=vel.at[:, pl.ds(place, 3), window, :],
            send_sem=halo_send.at[int(upward), step],
            recv_sem=halo_recv.at[int(upward), step],
            device_id={"depth": target},
            device_id_type=MESH,
        )

    def halo_arrival(step, upward):
        window = chunk_at(me, step)
        place = 0 if upward else slab + 3
        part = vel.at[:, pl.ds(place, 3), window, :]
        return pltpu.make_async_copy(part, part, halo_recv.at[int(upward), step])

    def edge_copy(component, rightward):
        target = (from_left if rightward else from_right).at[component]
        return pltpu.make_async_remote_copy(
            src_ref=edge.at[component],
            dst_ref=target,
            send_sem=edge_send.at[int(rightward), component],
            recv_sem=edge_recv.at[int(rightward), component],
            device_id={"tile": right if rightward else left},
            device_id_type=MESH,
        )

    def greet(level):
        for peer in (
            lax.rem(me + 2**level, depth_count),
            lax.rem(me + depth_count - 2**level, depth_count),
        ):
            pl.semaphore_signal(
                ready_sem.at[level], inc=1, device_id={"depth": peer}, device_id_type=MESH
            )

    pl.semaphore_wait(barrier, 2 + 2 * odd)
    for step in range(CHUNKS):
        for upward in (True, False):
            halo_copy(step, upward).start()
    greet(0)

    @pl.when(odd == 1)
    def _():
        for peer in (right, left):
            pl.semaphore_signal(tile_sem, inc=1, device_id={"tile": peer}, device_id_type=MESH)

    for component in range(3):
        loads[component].wait()

        def pack(part, carry):
            window = pl.ds(pl.multiple_of(part * 24, 8), 24)
            lane = lax.broadcasted_iota(jnp.int32, (24, lanes), 1)
            packed = jnp.zeros((24, lanes), jnp.float32)
            for plane in range(slab):
                turned = pltpu.roll(
                    vel[component, 3 + plane, window, :], (8 * plane + 3) % lanes, 1
                )
                packed = jnp.where(lane // 8 == plane, turned, packed)
            edge[component, window, :] = packed
            return carry

        lax.fori_loop(0, rows // 24, pack, 0)

        @pl.when(odd == 1)
        def _():
            for rightward in (True, False):
                edge_copy(component, rightward).start()

    pl.semaphore_wait(ready_sem.at[0], 2)
    greet(1)

    for load in loads[3:]:
        load.wait()
    diagonal = lax.broadcasted_iota(jnp.int32, (rows, rows), 0) == lax.broadcasted_iota(
        jnp.int32, (rows, rows), 1
    )
    column = jnp.sum(
        jnp.where(diagonal, jnp.broadcast_to(metric_in[...], (rows, rows)), 0.0),
        axis=1,
        keepdims=True,
    )
    metric[...] = jnp.broadcast_to(column, (rows, lanes))
    entries = map_in[...].astype(jnp.float32)
    steps = pltpu.roll(entries, lanes - 1, 1) - entries
    for channel in range(4):
        table[channel] = jnp.broadcast_to(entries[channel : channel + 1], (8, lanes))
        table[4 + channel] = jnp.broadcast_to(steps[channel : channel + 1], (8, lanes))

    def row_slopes(trip, carry):
        component = trip // 2
        for part in range(4):
            first = 2 * (4 * lax.rem(trip, 2) + part)
            both = jnp.concatenate([vel[component, 3 + first], vel[component, 4 + first]], axis=1)
            upper = both.astype(jnp.bfloat16)
            lower = (both - upper.astype(jnp.float32)).astype(jnp.bfloat16)
            slopes = jnp.dot(
                rowtab[...],
                jnp.concatenate([upper, lower], axis=0),
                preferred_element_type=jnp.float32,
            )
            for half in range(2):
                columns = slice(half * lanes, (half + 1) * lanes)
                high[component, first + half] = upper[:, columns]
                low[component, first + half] = lower[:, columns]
                dy[component, first + half] = slopes[:, columns] * metric[...]
        return carry

    lax.fori_loop(0, 3 * slab // 8, row_slopes, 0)

    pl.semaphore_wait(ready_sem.at[1], 2)
    greet(2)

    def lane_slopes(trip, carry):
        weights = jnp.concatenate([lanetab[...], lanetab[...]], axis=0)
        for part in range(4):
            plane = 4 * trip + part
            values = jnp.concatenate(
                [
                    high[:, plane].reshape(3 * rows, lanes),
                    low[:, plane].reshape(3 * rows, lanes),
                ],
                axis=1,
            )
            slopes = jnp.dot(values, weights, preferred_element_type=jnp.float32)
            dx[:, plane] = slopes.reshape(3, rows, lanes)
        return carry

    lax.fori_loop(0, slab // 4, lane_slopes, 0)

    pl.semaphore_wait(ready_sem.at[2], 2)
    greet(3)

    def without_lanes(plane, window):
        along = []
        for component in range(3):
            field = [vel[component, plane + k, window, :] for k in (0, 1, 2, 4, 5, 6)]
            along.append(
                45.0 * (field[3] - field[2]) - 9.0 * (field[4] - field[1]) + (field[5] - field[0])
            )
        normal = [dy[component, plane, window, :] for component in (1, 2)]
        twist = normal[1] - along[1]
        partial = normal[0] * normal[0] + along[2] * along[2] + 2.0 * (along[1] * normal[1])
        return partial, twist * twist, along[0]

    def inner_planes(part, carry):
        window = pl.ds(pl.multiple_of(part * 8, 8), 8)
        for plane in range(3, slab - 3):
            rest[plane, window, :], spin[plane, window, :], span[plane, window, :] = without_lanes(
                plane, window
            )
        return carry

    lax.fori_loop(0, rows // 8, inner_planes, 0)

    @pl.when(odd == 0)
    def _():
        pl.semaphore_wait(tile_sem, 2)
        for component in range(3):
            for rightward in (True, False):
                edge_copy(component, rightward).start()

    for component in range(3):
        for rightward in (True, False):
            edge_copy(component, rightward).wait_recv()

    wide_lane = lax.broadcasted_iota(jnp.int32, (3, rows, lanes), 2)
    halo = jnp.where(lax.rem(wide_lane, 8) < 3, from_left[...], from_right[...])
    halo_high = halo.astype(jnp.bfloat16)
    halo_low = (halo - halo_high.astype(jnp.float32)).astype(jnp.bfloat16)
    edge_parts[:, :lanes] = halo_high.reshape(3 * rows, lanes)
    edge_parts[:, lanes:] = halo_low.reshape(3 * rows, lanes)

    def edge_slopes(trip, carry):
        for part in range(2):
            pair = 2 * trip + part
            weights = jnp.concatenate([halotab[pair], halotab[pair]], axis=0)
            slopes = jnp.dot(edge_parts[...], weights, preferred_element_type=jnp.float32)
            for half in range(2):
                columns = slice(half * lanes, (half + 1) * lanes)
                dx[:, 2 * pair + half] += slopes[:, columns].reshape(3, rows, lanes)
        return carry

    lax.fori_loop(0, slab // 4, edge_slopes, 0)

    first_cell = me * slab

    def render(window):
        left_over = counts[window, :] - first_cell
        clear = jnp.ones((8, lanes), jnp.float32)
        total = jnp.zeros((8, lanes), jnp.float32)
        colour = [jnp.zeros((8, lanes), jnp.float32) for _ in range(3)]
        for plane in range(slab):
            if 3 <= plane < slab - 3:
                partial, square, along = (part[plane, window, :] for part in (rest, spin, span))
            else:
                partial, square, along = without_lanes(plane, window)
            stream = [dx[component, plane, window, :] for component in range(3)]
            normal = dy[0, plane, window, :]
            contraction = (
                partial
                + stream[0] * stream[0]
                + 2.0 * (normal * stream[1] + along * stream[2])
            )
            second, third = along - stream[2], stream[1] - normal
            square = square + second * second + third * third
            swirl = jnp.tanh(
                square * lax.rsqrt(jnp.maximum(square, 1e-30)) * (1.0 / (60.0 * VORTEX_SCALE))
            )
            scale = 0.5 * (lanes - 1)
            level = scale + scale * jnp.tanh(contraction * (-1.0 / (4.0 * 3600.0)))
            floor = jnp.minimum(jnp.floor(level), lanes - 2.0)
            fraction = level - floor
            bins = floor.astype(jnp.int32)
            values = [
                lookup(table[channel], bins) + fraction * lookup(table[4 + channel], bins)
                for channel in range(4)
            ]
            extinct = jnp.where(
                left_over > plane, values[0] * (OPTICAL_DEPTH / (slab * depth_count)), 0.0
            )
            opacity = extinct * (
                1.0 - extinct * (0.5 - extinct * (1.0 / 6.0 - extinct * (1.0 / 24.0)))
            )
            weight = clear * opacity
            clear = clear - weight
            total = total + extinct
            weight = weight * swirl
            colour = [colour[k] + weight * values[1 + k] for k in range(3)]
        return colour + [total]

    def piece_copy(owner):
        return pltpu.make_async_remote_copy(
            src_ref=pieces.at[owner],
            dst_ref=landed.at[me],
            send_sem=piece_send.at[owner],
            recv_sem=piece_recv.at[me],
            device_id={"depth": owner},
            device_id_type=MESH,
        )

    def render_chunk(step, carry):
        for upward in (True, False):
            halo_arrival(step, upward).wait()
        chunk = chunk_of(me, step)

        def render_rows(part, carry):
            window = pl.ds(pl.multiple_of(chunk * chunk_rows + part * 8, 8), 8)
            for channel, image in enumerate(render(window)):
                stage[channel, pl.ds(pl.multiple_of(part * 8, 8), 8), :] = image
            return carry

        lax.fori_loop(0, chunk_rows // 8, render_rows, 0)
        for row in range(3):
            for channel in range(4):
                spread = stage.at[channel][pl.ds(row, owners, stride=3), :]
                for owner in range(owners):
                    pieces[chunk * owners + owner, row, pl.ds(channel, 1), :] = spread[
                        owner : owner + 1
                    ]

        @pl.when(step == 0)
        def _():
            pl.semaphore_wait(ready_sem.at[3], 2)

        def send(place, carry):
            owner = chunk * owners + place

            @pl.when(owner != me)
            def _():
                piece_copy(owner).start()

            return carry

        lax.fori_loop(0, owners, send, 0)
        return carry

    lax.fori_loop(0, CHUNKS, render_chunk, 0)
    landed[me] = pieces[me]

    def receive(place, carry):
        @pl.when(place != me)
        def _():
            pltpu.make_async_copy(landed.at[place], landed.at[place], piece_recv.at[place]).wait()

        return carry

    lax.fori_loop(0, depth_count, receive, 0)

    before = jnp.zeros((3, 4, lanes), jnp.float32)
    image = jnp.zeros((3, 4, lanes), jnp.float32)
    for device in range(depth_count):
        part = landed[device]
        image = image + jnp.exp(-before) * part
        before = before + jnp.broadcast_to(landed[device, :, 3:4, :], (3, 4, lanes))
    channels = lax.broadcasted_iota(jnp.int32, (3, 4, lanes), 1)
    out_ref[...] = jnp.where(channels == 3, before, image)

    def sent(place, carry):
        @pl.when(place != me)
        def _():
            piece_copy(place).wait_send()

        return carry

    lax.fori_loop(0, depth_count, sent, 0)
    for component in range(3):
        for rightward in (True, False):
            edge_copy(component, rightward).wait_send()
    for step in range(CHUNKS):
        for upward in (True, False):
            halo_copy(step, upward).wait_send()


def per_device(depth_count, tile_count, velocity, metric, colour_map, counts):
    slab, rows, lanes = velocity.shape[1:]
    tables = stencil_tables(slab, rows, lanes)
    f32, bf16 = jnp.float32, jnp.bfloat16
    operands = (
        velocity,
        metric.reshape(1, rows),
        colour_map,
        counts,
        *(jnp.asarray(table) for table in tables),
    )
    block = (slab, rows, lanes)
    result = pl.pallas_call(
        functools.partial(kernel, depth_count, tile_count),
        out_shape=jax.ShapeDtypeStruct((rows // depth_count, 4, lanes), f32),
        in_specs=[pl.BlockSpec(memory_space=pl.ANY)] * len(operands),
        out_specs=pl.BlockSpec(memory_space=pltpu.VMEM),
        scratch_shapes=[
            pltpu.VMEM((3, slab + 6, rows, lanes), f32),
            pltpu.VMEM((3, *block), bf16),
            pltpu.VMEM((3, *block), bf16),
            pltpu.VMEM((3, *block), f32),
            pltpu.VMEM((3, *block), f32),
            pltpu.VMEM(block, f32),
            pltpu.VMEM(block, f32),
            pltpu.VMEM(block, f32),
            pltpu.VMEM((1, rows), f32),
            pltpu.VMEM((rows, lanes), f32),
            pltpu.VMEM(colour_map.shape, bf16),
            pltpu.VMEM((8, 8, lanes), f32),
            pltpu.VMEM((rows, lanes), jnp.int32),
            *(pltpu.VMEM(table.shape, bf16) for table in tables),
            pltpu.VMEM((3, rows, lanes), f32),
            pltpu.VMEM((3, rows, lanes), f32),
            pltpu.VMEM((3, rows, lanes), f32),
            pltpu.VMEM((3 * rows, 2 * lanes), bf16),
            pltpu.VMEM((4, rows // CHUNKS, lanes), f32),
            pltpu.VMEM((depth_count, rows // depth_count, 4, lanes), f32),
            pltpu.VMEM((depth_count, rows // depth_count, 4, lanes), f32),
            pltpu.SemaphoreType.DMA((9,)),
            pltpu.SemaphoreType.DMA((2, 3)),
            pltpu.SemaphoreType.DMA((2, 3)),
            pltpu.SemaphoreType.DMA((2, CHUNKS)),
            pltpu.SemaphoreType.DMA((2, CHUNKS)),
            pltpu.SemaphoreType.DMA((depth_count,)),
            pltpu.SemaphoreType.DMA((depth_count,)),
            pltpu.SemaphoreType.REGULAR((4,)),
            pltpu.SemaphoreType.REGULAR,
        ],
        compiler_params=pltpu.CompilerParams(
            collective_id=0, has_side_effects=True, vmem_limit_bytes=60 * 1024 * 1024
        ),
    )(*operands)
    channel = lax.broadcasted_iota(jnp.int32, result.shape, 1)
    return jnp.where(channel == 3, -jnp.expm1(-result), result).transpose(1, 0, 2)


def solution(mesh):
    in_specs = (P(None, "depth", None, "tile"), P(), P(), P(None, "tile"))
    out_specs = P(None, "depth", "tile")
    return jax.shard_map(
        functools.partial(per_device, mesh.shape["depth"], mesh.shape["tile"]),
        mesh=mesh,
        in_specs=in_specs,
        out_specs=out_specs,
        check_vma=False,
    )
```

```python
import functools

import jax
import jax.numpy as jnp
import numpy as np
from jax import lax
from jax.experimental import pallas as pl
from jax.experimental.pallas import tpu as pltpu
from jax.sharding import PartitionSpec as P

COEF = {1: 45.0, -1: -45.0, 2: -9.0, -2: 9.0, 3: 1.0, -3: -1.0}
VORTEX_SCALE = 4.0
OPTICAL_DEPTH = 4.0
CHUNKS = 4
TABLE_SCALE = 16384.0
MESH = pl.DeviceIdType.MESH
ALONG_LANES = lax.GatherDimensionNumbers(
    offset_dims=(),
    collapsed_slice_dims=(1,),
    start_index_map=(1,),
    operand_batching_dims=(0,),
    start_indices_batching_dims=(0,),
)


def stencil_tables(planes, rows, lanes):
    along_rows = np.zeros((rows, rows), np.float32)
    for row in range(rows):
        for offset, weight in COEF.items():
            if 0 <= row + offset < rows:
                along_rows[row, row + offset] = weight
    along_rows = np.concatenate([along_rows, along_rows], axis=1)
    along_lanes = np.zeros((lanes, lanes), np.float32)
    from_halo = np.zeros((planes // 2, lanes, 2 * lanes), np.float32)
    for lane in range(lanes):
        for offset, weight in COEF.items():
            source = lane + offset
            if 0 <= source < lanes:
                along_lanes[source, lane] = weight
                continue
            slot = source + 3 if source < 0 else source - lanes + 3
            for plane in range(planes):
                from_halo[plane // 2, 8 * plane + slot, plane % 2 * lanes + lane] = weight
    return tuple(table.astype(jnp.bfloat16) for table in (along_rows, along_lanes, from_halo))


def lookup(table, bins):
    return lax.gather(
        table,
        bins[..., None],
        ALONG_LANES,
        slice_sizes=(1, 1),
        mode=lax.GatherScatterMode.PROMISE_IN_BOUNDS,
    )


def kernel(
    depth_count,
    tile_count,
    vel_hbm,
    metric_hbm,
    map_hbm,
    counts_hbm,
    rowtab_hbm,
    lanetab_hbm,
    halotab_hbm,
    out_ref,
    vel,
    high,
    low,
    dx,
    dy,
    rest,
    spin,
    span,
    metric_in,
    metric,
    map_in,
    table,
    counts,
    rowtab,
    lanetab,
    halotab,
    edge,
    from_left,
    from_right,
    edge_parts,
    stage,
    pieces,
    landed,
    load_sem,
    edge_send,
    edge_recv,
    halo_send,
    halo_recv,
    piece_send,
    piece_recv,
    ready_sem,
    tile_sem,
):
    slab = vel_hbm.shape[1]
    rows, lanes = vel_hbm.shape[2:]
    chunk_rows = rows // CHUNKS
    owners = depth_count // CHUNKS
    me = lax.axis_index("depth")
    tile = lax.axis_index("tile")
    odd = lax.rem(tile, 2)
    up, down = lax.rem(me + 1, depth_count), lax.rem(me + depth_count - 1, depth_count)
    right, left = lax.rem(tile + 1, tile_count), lax.rem(tile + tile_count - 1, tile_count)

    barrier = pltpu.get_barrier_semaphore()

    def greet(semaphore, peers):
        for peer in peers:
            pl.semaphore_signal(semaphore, inc=1, device_id={"depth": peer}, device_id_type=MESH)

    def greet_level(level):
        greet(
            ready_sem.at[level],
            [lax.rem(me + shift, depth_count) for shift in (2**level, depth_count - 2**level)],
        )

    greet(barrier, [up, down])

    @pl.when(odd == 0)
    def _():
        for peer in (right, left):
            pl.semaphore_signal(barrier, inc=1, device_id={"tile": peer}, device_id_type=MESH)

    loads = [
        pltpu.make_async_copy(vel_hbm.at[c], vel.at[c, pl.ds(3, slab)], load_sem.at[c])
        for c in range(3)
    ]
    for place, (source, target) in enumerate(
        (
            (rowtab_hbm, rowtab),
            (metric_hbm, metric_in),
            (lanetab_hbm, lanetab),
            (map_hbm, map_in),
            (counts_hbm, counts),
            (halotab_hbm, halotab),
        )
    ):
        loads.append(pltpu.make_async_copy(source, target, load_sem.at[3 + place]))
    for load in loads:
        load.start()

    def chunk_of(device, step):
        own = device // owners
        return lax.rem(
            own + jnp.where(step == 0, 2, jnp.where(step == 1, 1, jnp.where(step == 2, 3, 0))),
            CHUNKS,
        )

    tiles = chunk_rows // 8

    def rows_at(device, place):
        first = chunk_of(device, place // tiles) * chunk_rows + lax.rem(place, tiles) * 8
        return pl.ds(pl.multiple_of(first, 8), 8)

    def halo_copy(place, upward):
        target = up if upward else down
        window = rows_at(target, place)
        source, landing = (slab - 3, 0) if upward else (0, slab + 3)
        return pltpu.make_async_remote_copy(
            src_ref=vel_hbm.at[:, pl.ds(source, 3), window, :],
            dst_ref=vel.at[:, pl.ds(landing, 3), window, :],
            send_sem=halo_send.at[int(upward), place],
            recv_sem=halo_recv.at[int(upward), place],
            device_id={"depth": target},
            device_id_type=MESH,
        )

    def halo_arrival(place, upward):
        landing = 0 if upward else slab + 3
        part = vel.at[:, pl.ds(landing, 3), rows_at(me, place), :]
        return pltpu.make_async_copy(part, part, halo_recv.at[int(upward), place])

    def edge_copy(component, rightward):
        target = (from_left if rightward else from_right).at[component]
        return pltpu.make_async_remote_copy(
            src_ref=edge.at[component],
            dst_ref=target,
            send_sem=edge_send.at[int(rightward), component],
            recv_sem=edge_recv.at[int(rightward), component],
            device_id={"tile": right if rightward else left},
            device_id_type=MESH,
        )

    pl.semaphore_wait(barrier, 2 + 2 * odd)

    def send_halo(place, carry):
        for upward in (True, False):
            halo_copy(place, upward).start()
        return carry

    lax.fori_loop(0, rows // 8, send_halo, 0)
    greet_level(0)

    @pl.when(odd == 1)
    def _():
        for peer in (right, left):
            pl.semaphore_signal(tile_sem, inc=1, device_id={"tile": peer}, device_id_type=MESH)

    for component in range(3):
        loads[component].wait()

        def pack(part, carry):
            window = pl.ds(pl.multiple_of(part * 24, 8), 24)
            lane = lax.broadcasted_iota(jnp.int32, (24, lanes), 1)
            packed = jnp.zeros((24, lanes), jnp.float32)
            for plane in range(slab):
                turned = pltpu.roll(
                    vel[component, 3 + plane, window, :], (8 * plane + 3) % lanes, 1
                )
                packed = jnp.where(lane // 8 == plane, turned, packed)
            edge[component, window, :] = packed
            return carry

        lax.fori_loop(0, rows // 24, pack, 0)

        @pl.when(odd == 1)
        def _():
            for rightward in (True, False):
                edge_copy(component, rightward).start()

    def answer():
        pl.semaphore_wait(tile_sem, 2)
        for component in range(3):
            for rightward in (True, False):
                edge_copy(component, rightward).start()

    pl.when((odd == 0) & (tile != 0))(answer)
    pl.semaphore_wait(ready_sem.at[0], 2)
    greet_level(1)

    for load in loads[3:]:
        load.wait()
    diagonal = lax.broadcasted_iota(jnp.int32, (rows, rows), 0) == lax.broadcasted_iota(
        jnp.int32, (rows, rows), 1
    )
    column = jnp.sum(
        jnp.where(diagonal, jnp.broadcast_to(metric_in[...], (rows, rows)), 0.0),
        axis=1,
        keepdims=True,
    )
    metric[...] = jnp.broadcast_to(column, (rows, lanes))
    entries = map_in[...].astype(jnp.float32) * TABLE_SCALE
    following = pltpu.roll(entries, lanes - 1, 1).astype(jnp.int32)
    both = entries.astype(jnp.int32) * 65536 + following
    for channel in range(4):
        table[channel] = jnp.broadcast_to(both[channel : channel + 1], (8, lanes))

    def row_slopes(trip, carry):
        component = trip // 2
        for part in range(4):
            first = 2 * (4 * lax.rem(trip, 2) + part)
            both = jnp.concatenate([vel[component, 3 + first], vel[component, 4 + first]], axis=1)
            upper = both.astype(jnp.bfloat16)
            lower = (both - upper.astype(jnp.float32)).astype(jnp.bfloat16)
            slopes = jnp.dot(
                rowtab[...],
                jnp.concatenate([upper, lower], axis=0),
                preferred_element_type=jnp.float32,
            )
            for half in range(2):
                columns = slice(half * lanes, (half + 1) * lanes)
                high[component, first + half] = upper[:, columns]
                low[component, first + half] = lower[:, columns]
                dy[component, first + half] = slopes[:, columns] * metric[...]
        return carry

    lax.fori_loop(0, 3 * slab // 8, row_slopes, 0)

    pl.semaphore_wait(ready_sem.at[1], 2)
    greet_level(2)
    pl.when(tile == 0)(answer)

    def lane_slopes(trip, carry):
        weights = jnp.concatenate([lanetab[...], lanetab[...]], axis=0)
        for part in range(4):
            plane = 4 * trip + part
            values = jnp.concatenate(
                [
                    high[:, plane].reshape(3 * rows, lanes),
                    low[:, plane].reshape(3 * rows, lanes),
                ],
                axis=1,
            )
            slopes = jnp.dot(values, weights, preferred_element_type=jnp.float32)
            dx[:, plane] = slopes.reshape(3, rows, lanes)
        return carry

    lax.fori_loop(0, slab // 4, lane_slopes, 0)

    pl.semaphore_wait(ready_sem.at[2], 2)
    greet_level(3)

    def without_lanes(plane, window):
        along = []
        for component in range(3):
            field = [vel[component, plane + k, window, :] for k in (0, 1, 2, 4, 5, 6)]
            along.append(
                45.0 * (field[3] - field[2]) - 9.0 * (field[4] - field[1]) + (field[5] - field[0])
            )
        normal = [dy[component, plane, window, :] for component in (1, 2)]
        twist = normal[1] - along[1]
        partial = normal[0] * normal[0] + along[2] * along[2] + 2.0 * (along[1] * normal[1])
        return partial, twist * twist, along[0]

    def inner_planes(part, carry):
        window = pl.ds(pl.multiple_of(part * 8, 8), 8)
        for plane in range(3, slab - 3):
            rest[plane, window, :], spin[plane, window, :], span[plane, window, :] = without_lanes(
                plane, window
            )
        return carry

    lax.fori_loop(0, rows // 8, inner_planes, 0)

    for component in range(3):
        for rightward in (True, False):
            edge_copy(component, rightward).wait_recv()

    wide_lane = lax.broadcasted_iota(jnp.int32, (3, rows, lanes), 2)
    halo = jnp.where(lax.rem(wide_lane, 8) < 3, from_left[...], from_right[...])
    halo_high = halo.astype(jnp.bfloat16)
    halo_low = (halo - halo_high.astype(jnp.float32)).astype(jnp.bfloat16)
    edge_parts[:, :lanes] = halo_high.reshape(3 * rows, lanes)
    edge_parts[:, lanes:] = halo_low.reshape(3 * rows, lanes)

    def edge_slopes(trip, carry):
        for part in range(2):
            pair = 2 * trip + part
            weights = jnp.concatenate([halotab[pair], halotab[pair]], axis=0)
            slopes = jnp.dot(edge_parts[...], weights, preferred_element_type=jnp.float32)
            for half in range(2):
                columns = slice(half * lanes, (half + 1) * lanes)
                dx[:, 2 * pair + half] += slopes[:, columns].reshape(3, rows, lanes)
        return carry

    lax.fori_loop(0, slab // 4, edge_slopes, 0)

    first_cell = me * slab

    def render(window):
        left_over = counts[window, :] - first_cell
        clear = jnp.ones((8, lanes), jnp.float32)
        total = jnp.zeros((8, lanes), jnp.float32)
        colour = [jnp.zeros((8, lanes), jnp.float32) for _ in range(3)]
        for plane in range(slab):
            if 3 <= plane < slab - 3:
                partial, square, along = (part[plane, window, :] for part in (rest, spin, span))
            else:
                partial, square, along = without_lanes(plane, window)
            stream = [dx[component, plane, window, :] for component in range(3)]
            normal = dy[0, plane, window, :]
            contraction = (
                partial
                + stream[0] * stream[0]
                + 2.0 * (normal * stream[1] + along * stream[2])
            )
            second, third = along - stream[2], stream[1] - normal
            square = square + second * second + third * third
            swirl = jnp.tanh(
                square * lax.rsqrt(jnp.maximum(square, 1e-30)) * (1.0 / (60.0 * VORTEX_SCALE))
            )
            scale = 0.5 * (lanes - 1)
            level = scale + scale * jnp.tanh(contraction * (-1.0 / (4.0 * 3600.0)))
            floor = jnp.minimum(jnp.floor(level), lanes - 2.0)
            fraction = level - floor
            bins = floor.astype(jnp.int32)
            remainder = 1.0 - fraction
            values = []
            for channel in range(4):
                pair = lookup(table[channel], bins)
                lower = lax.shift_right_logical(pair, 16).astype(jnp.float32)
                upper = (pair & 65535).astype(jnp.float32)
                values.append(remainder * lower + fraction * upper)
            extinct = jnp.where(
                left_over > plane, values[0] * (OPTICAL_DEPTH / (slab * depth_count * TABLE_SCALE)), 0.0
            )
            opacity = extinct * (
                1.0 - extinct * (0.5 - extinct * (1.0 / 6.0 - extinct * (1.0 / 24.0)))
            )
            weight = clear * opacity
            clear = clear - weight
            total = total + extinct
            weight = weight * swirl
            colour = [colour[k] + weight * values[1 + k] for k in range(3)]
        return [part * (1.0 / TABLE_SCALE) for part in colour] + [total]

    def piece_copy(owner):
        return pltpu.make_async_remote_copy(
            src_ref=pieces.at[owner],
            dst_ref=landed.at[me],
            send_sem=piece_send,
            recv_sem=piece_recv,
            device_id={"depth": owner},
            device_id_type=MESH,
        )

    def render_chunk(step, carry):
        chunk = chunk_of(me, step)

        def render_rows(part, carry):
            for upward in (True, False):
                halo_arrival(step * tiles + part, upward).wait()
            window = pl.ds(pl.multiple_of(chunk * chunk_rows + part * 8, 8), 8)
            for channel, image in enumerate(render(window)):
                stage[channel, pl.ds(pl.multiple_of(part * 8, 8), 8), :] = image
            return carry

        lax.fori_loop(0, chunk_rows // 8, render_rows, 0)
        for row in range(3):
            for channel in range(4):
                spread = stage.at[channel][pl.ds(row, owners, stride=3), :]
                for owner in range(owners):
                    pieces[chunk * owners + owner, row, pl.ds(channel, 1), :] = spread[
                        owner : owner + 1
                    ]

        @pl.when(step == 0)
        def _():
            pl.semaphore_wait(ready_sem.at[3], 2)

        def send(place, carry):
            owner = chunk * owners + place

            @pl.when(owner != me)
            def _():
                piece_copy(owner).start()

            return carry

        lax.fori_loop(0, owners, send, 0)
        return carry

    lax.fori_loop(0, CHUNKS, render_chunk, 0)
    landed[me] = pieces[me]

    others = landed.at[pl.ds(0, depth_count - 1)]
    pltpu.make_async_copy(others, others, piece_recv).wait()

    before = jnp.zeros((3, 4, lanes), jnp.float32)
    image = jnp.zeros((3, 4, lanes), jnp.float32)
    for device in range(depth_count):
        part = landed[device]
        image = image + jnp.exp(-before) * part
        before = before + jnp.broadcast_to(landed[device, :, 3:4, :], (3, 4, lanes))
    channels = lax.broadcasted_iota(jnp.int32, (3, 4, lanes), 1)
    out_ref[...] = jnp.where(channels == 3, before, image)

    pltpu.make_async_copy(others, others, piece_send).wait()
    for component in range(3):
        for rightward in (True, False):
            edge_copy(component, rightward).wait_send()

    def halo_sent(place, carry):
        for upward in (True, False):
            halo_copy(place, upward).wait_send()
        return carry

    lax.fori_loop(0, rows // 8, halo_sent, 0)


def per_device(depth_count, tile_count, velocity, metric, colour_map, counts):
    slab, rows, lanes = velocity.shape[1:]
    tables = stencil_tables(slab, rows, lanes)
    f32, bf16 = jnp.float32, jnp.bfloat16
    operands = (
        velocity,
        metric.reshape(1, rows),
        colour_map,
        counts,
        *(jnp.asarray(table) for table in tables),
    )
    block = (slab, rows, lanes)
    result = pl.pallas_call(
        functools.partial(kernel, depth_count, tile_count),
        out_shape=jax.ShapeDtypeStruct((rows // depth_count, 4, lanes), f32),
        in_specs=[pl.BlockSpec(memory_space=pl.ANY)] * len(operands),
        out_specs=pl.BlockSpec(memory_space=pltpu.VMEM),
        scratch_shapes=[
            pltpu.VMEM((3, slab + 6, rows, lanes), f32),
            pltpu.VMEM((3, *block), bf16),
            pltpu.VMEM((3, *block), bf16),
            pltpu.VMEM((3, *block), f32),
            pltpu.VMEM((3, *block), f32),
            pltpu.VMEM(block, f32),
            pltpu.VMEM(block, f32),
            pltpu.VMEM(block, f32),
            pltpu.VMEM((1, rows), f32),
            pltpu.VMEM((rows, lanes), f32),
            pltpu.VMEM(colour_map.shape, bf16),
            pltpu.VMEM((4, 8, lanes), jnp.int32),
            pltpu.VMEM((rows, lanes), jnp.int32),
            *(pltpu.VMEM(table.shape, bf16) for table in tables),
            pltpu.VMEM((3, rows, lanes), f32),
            pltpu.VMEM((3, rows, lanes), f32),
            pltpu.VMEM((3, rows, lanes), f32),
            pltpu.VMEM((3 * rows, 2 * lanes), bf16),
            pltpu.VMEM((4, rows // CHUNKS, lanes), f32),
            pltpu.VMEM((depth_count, rows // depth_count, 4, lanes), f32),
            pltpu.VMEM((depth_count, rows // depth_count, 4, lanes), f32),
            pltpu.SemaphoreType.DMA((9,)),
            pltpu.SemaphoreType.DMA((2, 3)),
            pltpu.SemaphoreType.DMA((2, 3)),
            pltpu.SemaphoreType.DMA((2, rows // 8)),
            pltpu.SemaphoreType.DMA((2, rows // 8)),
            pltpu.SemaphoreType.DMA,
            pltpu.SemaphoreType.DMA,
            pltpu.SemaphoreType.REGULAR((4,)),
            pltpu.SemaphoreType.REGULAR,
        ],
        compiler_params=pltpu.CompilerParams(
            collective_id=0, has_side_effects=True, vmem_limit_bytes=60 * 1024 * 1024
        ),
    )(*operands)
    channel = lax.broadcasted_iota(jnp.int32, result.shape, 1)
    return jnp.where(channel == 3, -jnp.expm1(-result), result).transpose(1, 0, 2)


def solution(mesh):
    in_specs = (P(None, "depth", None, "tile"), P(), P(), P(None, "tile"))
    out_specs = P(None, "depth", "tile")
    return jax.shard_map(
        functools.partial(per_device, mesh.shape["depth"], mesh.shape["tile"]),
        mesh=mesh,
        in_specs=in_specs,
        out_specs=out_specs,
        check_vma=False,
    )
```

```python
import functools

import jax
import jax.numpy as jnp
import numpy as np
from jax import lax
from jax.experimental import pallas as pl
from jax.experimental.pallas import tpu as pltpu
from jax.sharding import PartitionSpec as P

COEF = {1: 45.0, -1: -45.0, 2: -9.0, -2: 9.0, 3: 1.0, -3: -1.0}
VORTEX_SCALE = 4.0
OPTICAL_DEPTH = 4.0
CHUNKS = 4
TABLE_SCALE = 16384.0
MESH = pl.DeviceIdType.MESH
ALONG_LANES = lax.GatherDimensionNumbers(
    offset_dims=(),
    collapsed_slice_dims=(1,),
    start_index_map=(1,),
    operand_batching_dims=(0,),
    start_indices_batching_dims=(0,),
)


def stencil_tables(planes, rows, lanes):
    along_rows = np.zeros((rows, rows), np.float32)
    for row in range(rows):
        for offset, weight in COEF.items():
            if 0 <= row + offset < rows:
                along_rows[row, row + offset] = weight
    along_rows = np.concatenate([along_rows, along_rows], axis=1)
    along_lanes = np.zeros((lanes, lanes), np.float32)
    from_halo = np.zeros((planes // 2, lanes, 2 * lanes), np.float32)
    for lane in range(lanes):
        for offset, weight in COEF.items():
            source = lane + offset
            if 0 <= source < lanes:
                along_lanes[source, lane] = weight
                continue
            slot = source + 3 if source < 0 else source - lanes + 3
            for plane in range(planes):
                from_halo[plane // 2, 8 * plane + slot, plane % 2 * lanes + lane] = weight
    return tuple(table.astype(jnp.bfloat16) for table in (along_rows, along_lanes, from_halo))


def lookup(table, bins):
    return lax.gather(
        table,
        bins[..., None],
        ALONG_LANES,
        slice_sizes=(1, 1),
        mode=lax.GatherScatterMode.PROMISE_IN_BOUNDS,
    )


def kernel(
    depth_count,
    tile_count,
    vel_hbm,
    metric_hbm,
    map_hbm,
    counts_hbm,
    rowtab_hbm,
    lanetab_hbm,
    halotab_hbm,
    out_ref,
    vel,
    high,
    low,
    dx,
    dy,
    rest,
    spin,
    span,
    metric_in,
    metric,
    map_in,
    table,
    counts,
    rowtab,
    lanetab,
    halotab,
    edge,
    outgoing,
    from_left,
    from_right,
    edge_parts,
    stage,
    pieces,
    landed,
    load_sem,
    edge_send,
    edge_recv,
    halo_send,
    halo_recv,
    piece_send,
    piece_recv,
    ready_sem,
    tile_sem,
):
    slab = vel_hbm.shape[1]
    rows, lanes = vel_hbm.shape[2:]
    chunk_rows = rows // CHUNKS
    owners = depth_count // CHUNKS
    me = lax.axis_index("depth")
    tile = lax.axis_index("tile")
    odd = lax.rem(tile, 2)
    up, down = lax.rem(me + 1, depth_count), lax.rem(me + depth_count - 1, depth_count)
    right, left = lax.rem(tile + 1, tile_count), lax.rem(tile + tile_count - 1, tile_count)

    barrier = pltpu.get_barrier_semaphore()

    def greet(semaphore, peers):
        for peer in peers:
            pl.semaphore_signal(semaphore, inc=1, device_id={"depth": peer}, device_id_type=MESH)

    def greet_level(level):
        greet(
            ready_sem.at[level],
            [lax.rem(me + shift, depth_count) for shift in (2**level, depth_count - 2**level)],
        )

    greet(barrier, [up, down])

    @pl.when(odd == 0)
    def _():
        for peer in (right, left):
            pl.semaphore_signal(barrier, inc=1, device_id={"tile": peer}, device_id_type=MESH)

    loads = [
        pltpu.make_async_copy(vel_hbm.at[c], vel.at[c, pl.ds(3, slab)], load_sem.at[c])
        for c in range(3)
    ]
    for place, (source, target) in enumerate(
        (
            (rowtab_hbm, rowtab),
            (metric_hbm, metric_in),
            (lanetab_hbm, lanetab),
            (map_hbm, map_in),
            (counts_hbm, counts),
            (halotab_hbm, halotab),
        )
    ):
        loads.append(pltpu.make_async_copy(source, target, load_sem.at[3 + place]))
    for load in loads:
        load.start()

    def chunk_of(device, step):
        own = device // owners
        return lax.rem(
            own + jnp.where(step == 0, 2, jnp.where(step == 1, 1, jnp.where(step == 2, 3, 0))),
            CHUNKS,
        )

    tiles = chunk_rows // 8

    def rows_at(device, place):
        first = chunk_of(device, place // tiles) * chunk_rows + lax.rem(place, tiles) * 8
        return pl.ds(pl.multiple_of(first, 8), 8)

    def halo_copy(place, upward):
        target = up if upward else down
        window = rows_at(target, place)
        source, landing = (slab - 3, 0) if upward else (0, slab + 3)
        return pltpu.make_async_remote_copy(
            src_ref=vel_hbm.at[:, pl.ds(source, 3), window, :],
            dst_ref=vel.at[:, pl.ds(landing, 3), window, :],
            send_sem=halo_send.at[int(upward), place],
            recv_sem=halo_recv.at[int(upward), place],
            device_id={"depth": target},
            device_id_type=MESH,
        )

    def halo_arrival(place, upward):
        landing = 0 if upward else slab + 3
        part = vel.at[:, pl.ds(landing, 3), rows_at(me, place), :]
        return pltpu.make_async_copy(part, part, halo_recv.at[int(upward), place])

    def edge_copy(component, rightward):
        target = (from_left if rightward else from_right).at[component]
        return pltpu.make_async_remote_copy(
            src_ref=outgoing.at[int(rightward), component],
            dst_ref=target,
            send_sem=edge_send.at[int(rightward), component],
            recv_sem=edge_recv.at[int(rightward), component],
            device_id={"tile": right if rightward else left},
            device_id_type=MESH,
        )

    pl.semaphore_wait(barrier, 2 + 2 * odd)

    def send_halo(place, carry):
        for upward in (True, False):
            halo_copy(place, upward).start()
        return carry

    lax.fori_loop(0, rows // 8, send_halo, 0)
    greet_level(0)

    @pl.when(odd == 1)
    def _():
        for peer in (right, left):
            pl.semaphore_signal(tile_sem, inc=1, device_id={"tile": peer}, device_id_type=MESH)

    for component in range(3):
        loads[component].wait()

        def pack(part, carry):
            window = pl.ds(pl.multiple_of(part * 24, 8), 24)
            lane = lax.broadcasted_iota(jnp.int32, (24, lanes), 1)
            packed = jnp.zeros((24, lanes), jnp.float32)
            for plane in range(slab):
                turned = pltpu.roll(
                    vel[component, 3 + plane, window, :], (8 * plane + 3) % lanes, 1
                )
                packed = jnp.where(lane // 8 == plane, turned, packed)
            edge[component, window, :] = packed
            return carry

        lax.fori_loop(0, rows // 24, pack, 0)
        first, second = edge[component, : rows // 2], edge[component, rows // 2 :]
        slot = lax.rem(lax.broadcasted_iota(jnp.int32, first.shape, 1), 8)
        outgoing[1, component] = jnp.where(slot < 4, first, pltpu.roll(second, 4, 1))
        outgoing[0, component] = jnp.where(
            slot < 4, pltpu.roll(first, lanes - 3, 1), pltpu.roll(second, 1, 1)
        )

        @pl.when(odd == 1)
        def _():
            for rightward in (True, False):
                edge_copy(component, rightward).start()

    def answer():
        pl.semaphore_wait(tile_sem, 2)
        for component in range(3):
            for rightward in (True, False):
                edge_copy(component, rightward).start()

    pl.when((odd == 0) & (tile != 0))(answer)
    pl.semaphore_wait(ready_sem.at[0], 2)
    greet_level(1)

    for load in loads[3:]:
        load.wait()
    diagonal = lax.broadcasted_iota(jnp.int32, (rows, rows), 0) == lax.broadcasted_iota(
        jnp.int32, (rows, rows), 1
    )
    column = jnp.sum(
        jnp.where(diagonal, jnp.broadcast_to(metric_in[...], (rows, rows)), 0.0),
        axis=1,
        keepdims=True,
    )
    metric[...] = jnp.broadcast_to(column, (rows, lanes))
    entries = map_in[...].astype(jnp.float32) * TABLE_SCALE
    following = pltpu.roll(entries, lanes - 1, 1).astype(jnp.int32)
    both = entries.astype(jnp.int32) * 65536 + following
    for channel in range(4):
        table[channel] = jnp.broadcast_to(both[channel : channel + 1], (8, lanes))

    def row_slopes(trip, carry):
        component = trip // 2
        for part in range(4):
            first = 2 * (4 * lax.rem(trip, 2) + part)
            both = jnp.concatenate([vel[component, 3 + first], vel[component, 4 + first]], axis=1)
            upper = both.astype(jnp.bfloat16)
            lower = (both - upper.astype(jnp.float32)).astype(jnp.bfloat16)
            slopes = jnp.dot(
                rowtab[...],
                jnp.concatenate([upper, lower], axis=0),
                preferred_element_type=jnp.float32,
            )
            for half in range(2):
                columns = slice(half * lanes, (half + 1) * lanes)
                high[component, first + half] = upper[:, columns]
                low[component, first + half] = lower[:, columns]
                dy[component, first + half] = slopes[:, columns] * metric[...]
        return carry

    lax.fori_loop(0, 3 * slab // 8, row_slopes, 0)

    pl.semaphore_wait(ready_sem.at[1], 2)
    greet_level(2)
    pl.when(tile == 0)(answer)

    def lane_slopes(trip, carry):
        weights = jnp.concatenate([lanetab[...], lanetab[...]], axis=0)
        for part in range(4):
            plane = 4 * trip + part
            values = jnp.concatenate(
                [
                    high[:, plane].reshape(3 * rows, lanes),
                    low[:, plane].reshape(3 * rows, lanes),
                ],
                axis=1,
            )
            slopes = jnp.dot(values, weights, preferred_element_type=jnp.float32)
            dx[:, plane] = slopes.reshape(3, rows, lanes)
        return carry

    lax.fori_loop(0, slab // 4, lane_slopes, 0)

    pl.semaphore_wait(ready_sem.at[2], 2)
    greet_level(3)

    def without_lanes(plane, window):
        along = []
        for component in range(3):
            field = [vel[component, plane + k, window, :] for k in (0, 1, 2, 4, 5, 6)]
            along.append(
                45.0 * (field[3] - field[2]) - 9.0 * (field[4] - field[1]) + (field[5] - field[0])
            )
        normal = [dy[component, plane, window, :] for component in (1, 2)]
        twist = normal[1] - along[1]
        partial = normal[0] * normal[0] + along[2] * along[2] + 2.0 * (along[1] * normal[1])
        return partial, twist * twist, along[0]

    def inner_planes(part, carry):
        window = pl.ds(pl.multiple_of(part * 8, 8), 8)
        for plane in range(3, slab - 3):
            rest[plane, window, :], spin[plane, window, :], span[plane, window, :] = without_lanes(
                plane, window
            )
        return carry

    lax.fori_loop(0, rows // 8, inner_planes, 0)

    for component in range(3):
        for rightward in (True, False):
            edge_copy(component, rightward).wait_recv()

    for component in range(3):
        before, after = from_left[component], from_right[component]
        slot = lax.rem(lax.broadcasted_iota(jnp.int32, before.shape, 1), 8)
        upper_rows = jnp.where(slot < 3, before, pltpu.roll(after, 3, 1))
        lower_rows = jnp.where(
            slot < 3, pltpu.roll(before, lanes - 4, 1), pltpu.roll(after, lanes - 1, 1)
        )
        halo = jnp.concatenate([upper_rows, lower_rows], axis=0)
        halo_high = halo.astype(jnp.bfloat16)
        window = pl.ds(component * rows, rows)
        edge_parts[window, :lanes] = halo_high
        edge_parts[window, lanes:] = (halo - halo_high.astype(jnp.float32)).astype(jnp.bfloat16)

    def edge_slopes(trip, carry):
        for part in range(2):
            pair = 2 * trip + part
            weights = jnp.concatenate([halotab[pair], halotab[pair]], axis=0)
            slopes = jnp.dot(edge_parts[...], weights, preferred_element_type=jnp.float32)
            for half in range(2):
                columns = slice(half * lanes, (half + 1) * lanes)
                dx[:, 2 * pair + half] += slopes[:, columns].reshape(3, rows, lanes)
        return carry

    lax.fori_loop(0, slab // 4, edge_slopes, 0)

    first_cell = me * slab

    def render(window):
        left_over = counts[window, :] - first_cell
        clear = jnp.ones((8, lanes), jnp.float32)
        total = jnp.zeros((8, lanes), jnp.float32)
        colour = [jnp.zeros((8, lanes), jnp.float32) for _ in range(3)]
        for plane in range(slab):
            if 3 <= plane < slab - 3:
                partial, square, along = (part[plane, window, :] for part in (rest, spin, span))
            else:
                partial, square, along = without_lanes(plane, window)
            stream = [dx[component, plane, window, :] for component in range(3)]
            normal = dy[0, plane, window, :]
            contraction = (
                partial
                + stream[0] * stream[0]
                + 2.0 * (normal * stream[1] + along * stream[2])
            )
            second, third = along - stream[2], stream[1] - normal
            square = square + second * second + third * third
            swirl = jnp.tanh(
                square * lax.rsqrt(jnp.maximum(square, 1e-30)) * (1.0 / (60.0 * VORTEX_SCALE))
            )
            scale = 0.5 * (lanes - 1)
            level = scale + scale * jnp.tanh(contraction * (-1.0 / (4.0 * 3600.0)))
            floor = jnp.minimum(jnp.floor(level), lanes - 2.0)
            fraction = level - floor
            bins = floor.astype(jnp.int32)
            remainder = 1.0 - fraction
            values = []
            for channel in range(4):
                pair = lookup(table[channel], bins)
                lower = lax.shift_right_logical(pair, 16).astype(jnp.float32)
                upper = (pair & 65535).astype(jnp.float32)
                values.append(remainder * lower + fraction * upper)
            extinct = jnp.where(
                left_over > plane, values[0] * (OPTICAL_DEPTH / (slab * depth_count * TABLE_SCALE)), 0.0
            )
            opacity = extinct * (
                1.0 - extinct * (0.5 - extinct * (1.0 / 6.0 - extinct * (1.0 / 24.0)))
            )
            weight = clear * opacity
            clear = clear - weight
            total = total + extinct
            weight = weight * swirl
            colour = [colour[k] + weight * values[1 + k] for k in range(3)]
        return [part * (1.0 / TABLE_SCALE) for part in colour] + [total]

    def piece_copy(owner):
        return pltpu.make_async_remote_copy(
            src_ref=pieces.at[owner],
            dst_ref=landed.at[me],
            send_sem=piece_send,
            recv_sem=piece_recv,
            device_id={"depth": owner},
            device_id_type=MESH,
        )

    def render_chunk(step, carry):
        chunk = chunk_of(me, step)

        def render_rows(part, carry):
            for upward in (True, False):
                halo_arrival(step * tiles + part, upward).wait()
            window = pl.ds(pl.multiple_of(chunk * chunk_rows + part * 8, 8), 8)
            for channel, image in enumerate(render(window)):
                stage[channel, pl.ds(pl.multiple_of(part * 8, 8), 8), :] = image
            return carry

        lax.fori_loop(0, chunk_rows // 8, render_rows, 0)
        for row in range(3):
            for channel in range(4):
                spread = stage.at[channel][pl.ds(row, owners, stride=3), :]
                for owner in range(owners):
                    pieces[chunk * owners + owner, row, pl.ds(channel, 1), :] = spread[
                        owner : owner + 1
                    ]

        @pl.when(step == 0)
        def _():
            pl.semaphore_wait(ready_sem.at[3], 2)

        def send(place, carry):
            owner = chunk * owners + place

            @pl.when(owner != me)
            def _():
                piece_copy(owner).start()

            return carry

        lax.fori_loop(0, owners, send, 0)
        return carry

    lax.fori_loop(0, CHUNKS, render_chunk, 0)
    landed[me] = pieces[me]

    others = landed.at[pl.ds(0, depth_count - 1)]
    pltpu.make_async_copy(others, others, piece_recv).wait()

    before = jnp.zeros((3, 4, lanes), jnp.float32)
    image = jnp.zeros((3, 4, lanes), jnp.float32)
    for device in range(depth_count):
        part = landed[device]
        image = image + jnp.exp(-before) * part
        before = before + jnp.broadcast_to(landed[device, :, 3:4, :], (3, 4, lanes))
    channels = lax.broadcasted_iota(jnp.int32, (3, 4, lanes), 1)
    out_ref[...] = jnp.where(channels == 3, before, image)

    pltpu.make_async_copy(others, others, piece_send).wait()
    for component in range(3):
        for rightward in (True, False):
            edge_copy(component, rightward).wait_send()

    def halo_sent(place, carry):
        for upward in (True, False):
            halo_copy(place, upward).wait_send()
        return carry

    lax.fori_loop(0, rows // 8, halo_sent, 0)


def per_device(depth_count, tile_count, velocity, metric, colour_map, counts):
    slab, rows, lanes = velocity.shape[1:]
    tables = stencil_tables(slab, rows, lanes)
    f32, bf16 = jnp.float32, jnp.bfloat16
    operands = (
        velocity,
        metric.reshape(1, rows),
        colour_map,
        counts,
        *(jnp.asarray(table) for table in tables),
    )
    block = (slab, rows, lanes)
    result = pl.pallas_call(
        functools.partial(kernel, depth_count, tile_count),
        out_shape=jax.ShapeDtypeStruct((rows // depth_count, 4, lanes), f32),
        in_specs=[pl.BlockSpec(memory_space=pl.ANY)] * len(operands),
        out_specs=pl.BlockSpec(memory_space=pltpu.VMEM),
        scratch_shapes=[
            pltpu.VMEM((3, slab + 6, rows, lanes), f32),
            pltpu.VMEM((3, *block), bf16),
            pltpu.VMEM((3, *block), bf16),
            pltpu.VMEM((3, *block), f32),
            pltpu.VMEM((3, *block), f32),
            pltpu.VMEM(block, f32),
            pltpu.VMEM(block, f32),
            pltpu.VMEM(block, f32),
            pltpu.VMEM((1, rows), f32),
            pltpu.VMEM((rows, lanes), f32),
            pltpu.VMEM(colour_map.shape, bf16),
            pltpu.VMEM((4, 8, lanes), jnp.int32),
            pltpu.VMEM((rows, lanes), jnp.int32),
            *(pltpu.VMEM(table.shape, bf16) for table in tables),
            pltpu.VMEM((3, rows, lanes), f32),
            pltpu.VMEM((2, 3, rows // 2, lanes), f32),
            pltpu.VMEM((3, rows // 2, lanes), f32),
            pltpu.VMEM((3, rows // 2, lanes), f32),
            pltpu.VMEM((3 * rows, 2 * lanes), bf16),
            pltpu.VMEM((4, rows // CHUNKS, lanes), f32),
            pltpu.VMEM((depth_count, rows // depth_count, 4, lanes), f32),
            pltpu.VMEM((depth_count, rows // depth_count, 4, lanes), f32),
            pltpu.SemaphoreType.DMA((9,)),
            pltpu.SemaphoreType.DMA((2, 3)),
            pltpu.SemaphoreType.DMA((2, 3)),
            pltpu.SemaphoreType.DMA((2, rows // 8)),
            pltpu.SemaphoreType.DMA((2, rows // 8)),
            pltpu.SemaphoreType.DMA,
            pltpu.SemaphoreType.DMA,
            pltpu.SemaphoreType.REGULAR((4,)),
            pltpu.SemaphoreType.REGULAR,
        ],
        compiler_params=pltpu.CompilerParams(
            collective_id=0, has_side_effects=True, vmem_limit_bytes=60 * 1024 * 1024
        ),
    )(*operands)
    channel = lax.broadcasted_iota(jnp.int32, result.shape, 1)
    return jnp.where(channel == 3, -jnp.expm1(-result), result).transpose(1, 0, 2)


def solution(mesh):
    in_specs = (P(None, "depth", None, "tile"), P(), P(), P(None, "tile"))
    out_specs = P(None, "depth", "tile")
    return jax.shard_map(
        functools.partial(per_device, mesh.shape["depth"], mesh.shape["tile"]),
        mesh=mesh,
        in_specs=in_specs,
        out_specs=out_specs,
        check_vma=False,
    )
```
